32 devices in a mesh: shard: 4 (over y, x), ctx: 4 (over z), tp: 2 (over core).
Axes of the slice: x: 2, y: 2, z: 4, core: 2. Of those that a mesh axis runs over, the one named last changes fastest.
Arguments:
- inputs: bfloat16 [4096, 1024], P(('shard', 'ctx')), may hold values from -6 to 6
- lengths: int32 [4, 3], P('shard'), may hold values from 1 to 768, 1024 in all within a row
- cotangent: bfloat16 [4096, 1024], P(('shard', 'ctx')), may hold values from -6 to 6
- w_qkv: bfloat16 [3, 1024, 1024], P(None, 'shard', 'tp'), may hold values from -0.1875 to 0.1875
- w_out: bfloat16 [1024, 1024], P('tp', 'shard'), may hold values from -0.5 to 0.5
- w_fc: bfloat16 [1024, 4096], P('shard', 'tp'), may hold values from -0.1875 to 0.1875
- w_proj: bfloat16 [4096, 1024], P('tp', 'shard'), may hold values from -0.09375 to 0.09375
- b_qv: float32 [2, 1024], P(None, 'tp'), may hold values from -3 to 3
- b_out: float32 [1024], replicated, may hold values from -2 to 2
- b_fc: float32 [4096], P('tp'), may hold values from -3 to 3
- b_proj: float32 [1024], replicated, may hold values from -2 to 2
- ln1_gain: float32 [1024], replicated, may hold values from 0.25 to 1.75
- ln1_bias: float32 [1024], replicated, may hold values from -2 to 2
- ln2_gain: float32 [1024], replicated, may hold values from 0.25 to 1.75
- ln2_bias: float32 [1024], replicated, may hold values from -2 to 2
Outputs:
- outputs: bfloat16 [4096, 1024], P(('shard', 'ctx'))
- grad_inputs: bfloat16 [4096, 1024], P(('shard', 'ctx'))
- grad_w_qkv: float32 [3, 1024, 1024], P(None, 'shard', 'tp')
- grad_w_out: float32 [1024, 1024], P('tp', 'shard')
- grad_w_fc: float32 [1024, 4096], P('shard', 'tp')
- grad_w_proj: float32 [4096, 1024], P('tp', 'shard')
- grad_b_qv: float32 [2, 1024], P(None, 'tp')
- grad_b_out: float32 [1024], replicated
- grad_b_fc: float32 [4096], P('tp')
- grad_b_proj: float32 [1024], replicated
- grad_ln1_gain: float32 [1024], replicated
- grad_ln1_bias: float32 [1024], replicated
- grad_ln2_gain: float32 [1024], replicated
- grad_ln2_bias: float32 [1024], replicated
The draws below stay inside these ranges and needn't reach their ends.
Inputs may be any that keep to these rules, and one draw needn't show every extreme that they name: Each row holds the lengths of one shard's 3 sequences in order; they sum to 1024, and the largest is 768.
All inputs are finite; a program needn't handle non-finite values.
Results may differ from the reference program's by a relative error of at most 0.02.
Values may be sent and summed in bfloat16 or wider, within the bound.
A program may use at most 128 MiB of HBM per device.

```python
import math
import jax
import jax.numpy as jnp
import numpy as np
from jax import lax

D = 1024
HEADS = 16
HEAD_DIM = 64
FF = 4096
SEQS = 3
BLOCK = 1024
SEQ_MOST = 768
SHARDS = 4
TOKENS = 4096


def shard_levels(stream_key, dims, cuts, least, largest):
    factor_of, own = 1.0, jax.random.fold_in(stream_key, 6)
    for dim, parts in cuts:
        heights = jnp.exp(jax.random.uniform(jax.random.fold_in(own, dim), (parts,), jnp.float32, least / len(cuts), largest / len(cuts)))
        factor_of = factor_of * jnp.repeat(heights, dims[dim] // parts).reshape([-1 if axis == dim else 1 for axis in range(len(dims))])
    return factor_of


def length_profile(count, total, reach, slope):
    loads = [(1 << 20) // math.isqrt(rank ** slope) + 1 for rank in range(2, count + 1)]
    surplus, holding = total - reach - (count - 1), [1] * (count - 1)
    while surplus > 0:
        movable = [i for i in range(count - 1) if holding[i] < reach]
        mass, remaining = sum([loads[i] for i in movable]), surplus
        for i in movable:
            addition = min(reach - holding[i], max(1, remaining * loads[i] // mass), surplus)
            holding[i] = holding[i] + addition
            surplus = surplus - addition
    return np.array([reach] + holding)


def uneven_parts(rng, amount, total, reach, skew):
    if amount == 2:
        one = jax.random.randint(rng, (), max(1, total - reach), min(reach, total - 1) + 1)
        return jnp.stack([one, total - one])
    tallies = jnp.asarray(length_profile(amount, total, reach, skew), jnp.int32)
    pairs = (amount - 1) // 2
    donor, sink = tallies[1:1 + 2 * pairs:2], tallies[2:2 + 2 * pairs:2]
    slack = jnp.minimum(donor - 1, reach - sink)
    passed = jax.random.randint(jax.random.fold_in(rng, 1), (pairs,), 0, 1 << 20) % (slack + 1)
    tallies = tallies.at[1:1 + 2 * pairs:2].set(donor - passed).at[2:2 + 2 * pairs:2].set(sink + passed)
    return tallies[jax.random.permutation(jax.random.fold_in(rng, 2), amount)]


def noise(key, dims, deviation, limit, shards=(), held_as=jnp.bfloat16):
    result = jax.random.normal(key, dims, jnp.float32) * deviation
    if len(shards) > 0:
        result = shard_levels(key, dims, shards, -0.22, 0.18) * result
    return jnp.clip(result, min=-limit, max=limit).astype(held_as)


def setup_inputs(seed: int = 0) -> dict:
    splits = jax.random.split(jax.random.key(seed), 16)
    inputs = noise(splits[0], (TOKENS, D), 1.0, 6.0, ((0, 16),))
    lengths = jax.vmap(lambda own: uneven_parts(own, SEQS, BLOCK, SEQ_MOST, 2))(jax.random.split(splits[1], SHARDS)).reshape((SHARDS, SEQS)).astype(jnp.int32)
    cotangent = noise(splits[2], (TOKENS, D), 1.0, 6.0, ((0, 16),))
    w_qkv = noise(splits[3], (3, D, D), D ** -0.5, 0.1875, ((1, 4), (2, 2)))
    w_out = noise(splits[4], (D, D), (D // 8) ** -0.5, 0.5, ((0, 2), (1, 4)))
    w_fc = noise(splits[5], (D, FF), D ** -0.5, 0.1875, ((0, 4), (1, 2)))
    w_proj = noise(splits[6], (FF, D), FF ** -0.5, 0.09375, ((0, 2), (1, 4)))
    b_qv = noise(splits[7], (2, D), 0.5, 3.0, ((1, 2),), jnp.float32)
    b_out = noise(splits[8], (D,), 0.3, 2.0, (), jnp.float32)
    b_fc = noise(splits[9], (FF,), 0.5, 3.0, ((0, 2),), jnp.float32)
    b_proj = noise(splits[10], (D,), 0.3, 2.0, (), jnp.float32)
    ln1_gain = jnp.clip(1.0 + 0.15 * jax.random.normal(splits[11], (D,), jnp.float32), 0.25, 1.75)
    ln1_bias = noise(splits[12], (D,), 0.3, 2.0, (), jnp.float32)
    ln2_gain = jnp.clip(1.0 + 0.15 * jax.random.normal(splits[13], (D,), jnp.float32), 0.25, 1.75)
    ln2_bias = noise(splits[14], (D,), 0.3, 2.0, (), jnp.float32)
    return dict(inputs=inputs, lengths=lengths, cotangent=cotangent, w_qkv=w_qkv, w_out=w_out, w_fc=w_fc, w_proj=w_proj, b_qv=b_qv, b_out=b_out, b_fc=b_fc, b_proj=b_proj, ln1_gain=ln1_gain, ln1_bias=ln1_bias, ln2_gain=ln2_gain, ln2_bias=ln2_bias)


def layer_norm(values, gain, shift):
    mean = lax.optimization_barrier(jnp.mean(values, axis=-1, keepdims=True))
    centred = values - mean
    spread = lax.optimization_barrier(jnp.mean(centred * centred, axis=-1, keepdims=True))
    return centred * lax.rsqrt(spread + 1e-05) * gain + shift

def gelu_tanh(values):
    return 0.5 * values * (1.0 + jnp.tanh(0.7978845608028654 * (values + 0.044715 * values * values * values)))

def segment_ids(lengths, count):
    ends = jnp.cumsum(lengths).astype(jnp.int32)
    places = jnp.arange(count, dtype=jnp.int32)
    return lax.optimization_barrier(jnp.sum((places[:, None] >= ends[None, :]).astype(jnp.int32), axis=1)).astype(jnp.int32)

def dot32(left, right):
    return jnp.dot(left, right, preferred_element_type=jnp.float32)

def reference(inputs, lengths, cotangent, w_qkv, w_out, w_fc, w_proj, b_qv, b_out, b_fc, b_proj, ln1_gain, ln1_bias, ln2_gain, ln2_bias):
    bf = jnp.bfloat16
    f32 = jnp.float32
    x_all = inputs.reshape(SHARDS, BLOCK, D)
    dy_all = cotangent.reshape(SHARDS, BLOCK, D)

    def group(carry, data):
        x_rows, lens, d_out = data
        seg = segment_ids(lens, BLOCK)
        places = jnp.arange(BLOCK, dtype=jnp.int32)
        allowed = (places[None, :] <= places[:, None]) & (seg[None, :] == seg[:, None])
        x_f = x_rows.astype(f32)
        normed1 = layer_norm(x_f, ln1_gain, ln1_bias).astype(bf)
        query = ((dot32(normed1, w_qkv[0]) + b_qv[0]) * 0.125).astype(bf)
        key = dot32(normed1, w_qkv[1]).astype(bf)
        value = (dot32(normed1, w_qkv[2]) + b_qv[1]).astype(bf)
        q3 = query.reshape(BLOCK, HEADS, HEAD_DIM).astype(f32)
        k3 = key.reshape(BLOCK, HEADS, HEAD_DIM).astype(f32)
        v3 = value.reshape(BLOCK, HEADS, HEAD_DIM).astype(f32)
        scores = jnp.einsum('rhd,nhd->hrn', q3, k3)
        weights = jnp.where(allowed[None], jnp.exp(scores), 0.0)
        total = lax.optimization_barrier(jnp.sum(weights, axis=2))
        log_total = jnp.log(total)
        acc = jnp.einsum('hrn,nhd->hrd', weights.astype(bf).astype(f32), v3)
        attended = (acc / total[:, :, None]).transpose(1, 0, 2).reshape(BLOCK, D).astype(bf)
        hidden = x_f + dot32(attended, w_out) + b_out
        normed2 = layer_norm(hidden, ln2_gain, ln2_bias).astype(bf)
        pre = dot32(normed2, w_fc) + b_fc
        act = gelu_tanh(pre).astype(bf)
        outputs = (hidden + dot32(act, w_proj) + b_proj).astype(bf)
        grad_f = d_out.astype(f32)
        g_bproj = lax.optimization_barrier(jnp.sum(grad_f, axis=0))
        g_proj = dot32(act.T, d_out)
        d_act = dot32(d_out, w_proj.T)
        gelu_back = jax.vjp(gelu_tanh, pre)[1]
        d_pre = gelu_back(d_act)[0]
        g_bfc = lax.optimization_barrier(jnp.sum(d_pre, axis=0))
        d_pre_b = d_pre.astype(bf)
        g_fc = dot32(normed2.T, d_pre_b)
        d_normed2 = dot32(d_pre_b, w_fc.T)
        norm_back2 = jax.vjp(layer_norm, hidden, ln2_gain, ln2_bias)[1]
        d_norm2, g_ln2g, g_ln2b = norm_back2(d_normed2)
        d_hidden = grad_f + d_norm2
        g_bout = lax.optimization_barrier(jnp.sum(d_hidden, axis=0))
        d_hidden_b = d_hidden.astype(bf)
        g_out = dot32(attended.T, d_hidden_b)
        d_attended = dot32(d_hidden_b, w_out.T).astype(bf)
        da3 = d_attended.reshape(BLOCK, HEADS, HEAD_DIM).astype(f32)
        at3 = attended.reshape(BLOCK, HEADS, HEAD_DIM).astype(f32)
        delta = jnp.einsum('rhd,rhd->hr', da3, at3)
        probs = jnp.where(allowed[None], jnp.exp(scores - log_total[:, :, None]), 0.0)
        d_value = jnp.einsum('hrn,rhd->nhd', probs.astype(bf).astype(f32), da3).reshape(BLOCK, D)
        d_probs = jnp.einsum('rhd,nhd->hrn', da3, v3)
        d_scores_b = (probs * (d_probs - delta[:, :, None])).astype(bf).astype(f32)
        d_query = jnp.einsum('hrn,nhd->rhd', d_scores_b, k3).reshape(BLOCK, D) * 0.125
        d_key = jnp.einsum('hrn,rhd->nhd', d_scores_b, q3).reshape(BLOCK, D)
        g_bqv = jnp.stack([lax.optimization_barrier(jnp.sum(d_query, axis=0)), lax.optimization_barrier(jnp.sum(d_value, axis=0))])
        d_query_b = d_query.astype(bf)
        d_key_b = d_key.astype(bf)
        d_value_b = d_value.astype(bf)
        g_qkv = jnp.stack([dot32(normed1.T, d_query_b), dot32(normed1.T, d_key_b), dot32(normed1.T, d_value_b)])
        d_normed1 = dot32(d_query_b, w_qkv[0].T) + dot32(d_key_b, w_qkv[1].T) + dot32(d_value_b, w_qkv[2].T)
        norm_back1 = jax.vjp(layer_norm, x_f, ln1_gain, ln1_bias)[1]
        d_norm1, g_ln1g, g_ln1b = norm_back1(d_normed1)
        grad_inputs = (d_hidden + d_norm1).astype(bf)
        terms = (g_qkv, g_out, g_fc, g_proj, g_bqv, g_bout, g_bfc, g_bproj, g_ln1g, g_ln1b, g_ln2g, g_ln2b)
        carry = tuple((c + t for c, t in zip(carry, terms)))
        return (carry, (outputs, grad_inputs))
    init = (jnp.zeros((3, D, D), f32), jnp.zeros((D, D), f32), jnp.zeros((D, FF), f32), jnp.zeros((FF, D), f32), jnp.zeros((2, D), f32), jnp.zeros((D,), f32), jnp.zeros((FF,), f32), jnp.zeros((D,), f32), jnp.zeros((D,), f32), jnp.zeros((D,), f32), jnp.zeros((D,), f32), jnp.zeros((D,), f32))
    sums, (outs, grads_in) = lax.scan(group, init, (x_all, lengths, dy_all))
    return (outs.reshape(TOKENS, D), grads_in.reshape(TOKENS, D), sums[0], sums[1], sums[2], sums[3], sums[4], sums[5], sums[6], sums[7], sums[8], sums[9], sums[10], sums[11])
```

```python
import jax
import jax.numpy as jnp
from jax import lax
from jax.experimental import pallas as pl
from jax.experimental.pallas import tpu as pltpu
from jax.sharding import PartitionSpec as P

HEAD_DIM = 64


def layer_norm(values, gain, shift):
    mean = jnp.mean(values, axis=-1, keepdims=True)
    centred = values - mean
    spread = jnp.mean(centred * centred, axis=-1, keepdims=True)
    return centred * lax.rsqrt(spread + 1e-05) * gain + shift


def gelu_tanh(values):
    return (
        0.5
        * values
        * (1.0 + jnp.tanh(0.7978845608028654 * (values + 0.044715 * values * values * values)))
    )


def segment_ids(lengths, count):
    ends = jnp.cumsum(lengths)
    places = jnp.arange(count, dtype=jnp.int32)
    return jnp.sum((places[:, None] >= ends[None, :]).astype(jnp.int32), axis=1)


def dot32(left, right):
    return jnp.dot(left, right, preferred_element_type=jnp.float32)


def on_device_general(
    inputs,
    lengths,
    cotangent,
    w_qkv,
    w_out,
    w_fc,
    w_proj,
    b_qv,
    b_out,
    b_fc,
    b_proj,
    ln1_gain,
    ln1_bias,
    ln2_gain,
    ln2_bias,
):
    bf = jnp.bfloat16
    f32 = jnp.float32
    rows = inputs.shape[0]
    parts = lax.axis_size("ctx")
    block = rows * parts
    local_width = b_qv.shape[1]
    local_heads = local_width // HEAD_DIM
    seg_all = segment_ids(lengths[0], block)
    first = lax.axis_index("ctx") * rows
    q_pos = first + jnp.arange(rows, dtype=jnp.int32)
    q_seg = lax.dynamic_slice_in_dim(seg_all, first, rows)
    wq_all, wo_all, wfc_all, wproj_all = (
        lax.all_gather(w_qkv, "shard", axis=1, tiled=True),
        lax.all_gather(w_out, "shard", axis=1, tiled=True),
        lax.all_gather(w_fc, "shard", axis=0, tiled=True),
        lax.all_gather(w_proj, "shard", axis=1, tiled=True),
    )
    x_f = inputs.astype(f32)
    normed1 = layer_norm(x_f, ln1_gain, ln1_bias).astype(bf)
    query = ((dot32(normed1, wq_all[0]) + b_qv[0]) * 0.125).astype(bf)
    key = dot32(normed1, wq_all[1]).astype(bf)
    value = (dot32(normed1, wq_all[2]) + b_qv[1]).astype(bf)
    q3 = query.reshape(rows, local_heads, HEAD_DIM)

    def allowed_for(start, count):
        k_pos = start + jnp.arange(count, dtype=jnp.int32)
        k_seg = lax.dynamic_slice_in_dim(seg_all, start, count)
        return (k_pos[None, :] <= q_pos[:, None]) & (k_seg[None, :] == q_seg[:, None])

    k_piece = lax.all_gather(key, "ctx", axis=0, tiled=True)
    v_piece = lax.all_gather(value, "ctx", axis=0, tiled=True)
    count = k_piece.shape[0]
    allowed = allowed_for(jnp.int32(0), count)
    scores = jnp.einsum(
        "rhd,nhd->hrn",
        q3,
        k_piece.reshape(count, local_heads, HEAD_DIM),
        preferred_element_type=f32,
    )
    weights = jnp.where(allowed[None], jnp.exp(scores), 0.0)
    total = jnp.sum(weights, axis=2)
    acc = jnp.einsum(
        "hrn,nhd->hrd",
        weights.astype(bf),
        v_piece.reshape(count, local_heads, HEAD_DIM),
        preferred_element_type=f32,
    )
    total, acc = (total, acc)
    log_total = jnp.log(total)
    attended = (acc / total[:, :, None]).transpose(1, 0, 2).reshape(rows, local_width).astype(bf)
    mixed = lax.psum(dot32(attended, wo_all).astype(jnp.bfloat16), "tp").astype(jnp.float32)
    hidden = x_f + mixed + b_out
    normed2 = layer_norm(hidden, ln2_gain, ln2_bias).astype(bf)
    pre = dot32(normed2, wfc_all) + b_fc
    act = gelu_tanh(pre).astype(bf)
    mlp_total = lax.psum(dot32(act, wproj_all).astype(jnp.bfloat16), "tp").astype(jnp.float32)
    outputs = (hidden + mlp_total + b_proj).astype(bf)
    wq_back, wo_back, wfc_back, wproj_back = (
        lax.all_gather(w_qkv, "shard", axis=1, tiled=True),
        lax.all_gather(w_out, "shard", axis=1, tiled=True),
        lax.all_gather(w_fc, "shard", axis=0, tiled=True),
        lax.all_gather(w_proj, "shard", axis=1, tiled=True),
    )
    grad_f = cotangent.astype(f32)
    g_bproj = jnp.sum(grad_f, axis=0)
    g_proj = dot32(act.T, cotangent)
    d_act = dot32(cotangent, wproj_back.T)
    gelu_back = jax.vjp(gelu_tanh, pre)[1]
    d_pre = gelu_back(d_act)[0]
    g_bfc = jnp.sum(d_pre, axis=0)
    d_pre_b = d_pre.astype(bf)
    g_fc = dot32(normed2.T, d_pre_b)
    d_normed2 = lax.psum(dot32(d_pre_b, wfc_back.T).astype(jnp.bfloat16), "tp").astype(jnp.float32)
    norm_back2 = jax.vjp(layer_norm, hidden, ln2_gain, ln2_bias)[1]
    d_norm2, g_ln2g, g_ln2b = norm_back2(d_normed2)
    d_hidden = grad_f + d_norm2
    g_bout = jnp.sum(d_hidden, axis=0)
    d_hidden_b = d_hidden.astype(bf)
    g_out = dot32(attended.T, d_hidden_b)
    d_attended = dot32(d_hidden_b, wo_back.T).astype(bf)
    da3 = d_attended.reshape(rows, local_heads, HEAD_DIM)
    at3 = attended.reshape(rows, local_heads, HEAD_DIM)
    delta = jnp.einsum("rhd,rhd->hr", da3, at3, preferred_element_type=f32)
    key_all, value_all = (
        lax.all_gather(key, "ctx", axis=0, tiled=True),
        lax.all_gather(value, "ctx", axis=0, tiled=True),
    )
    key_blocks = key_all.reshape(parts, rows, local_heads, HEAD_DIM)
    value_blocks = value_all.reshape(parts, rows, local_heads, HEAD_DIM)
    starts = jnp.arange(parts, dtype=jnp.int32) * rows

    def back_piece(d_query_acc, inputs_piece):
        k_piece, v_piece, start = inputs_piece
        allowed = allowed_for(start, rows)
        scores = jnp.einsum("rhd,nhd->hrn", q3, k_piece, preferred_element_type=f32)
        probs = jnp.where(allowed[None], jnp.exp(scores - log_total[:, :, None]), 0.0)
        d_v = jnp.einsum("hrn,rhd->nhd", probs.astype(bf), da3, preferred_element_type=f32)
        d_probs = jnp.einsum("rhd,nhd->hrn", da3, v_piece, preferred_element_type=f32)
        d_scores_b = (probs * (d_probs - delta[:, :, None])).astype(bf)
        d_query_acc = d_query_acc + jnp.einsum(
            "hrn,nhd->rhd", d_scores_b, k_piece, preferred_element_type=f32
        )
        d_k = jnp.einsum("hrn,rhd->nhd", d_scores_b, q3, preferred_element_type=f32)
        return (d_query_acc, (d_k.reshape(rows, local_width), d_v.reshape(rows, local_width)))

    zero_query = jnp.zeros((rows, local_heads, HEAD_DIM), f32)
    d_query_acc, (d_key_terms, d_value_terms) = lax.scan(
        back_piece, zero_query, (key_blocks, value_blocks, starts)
    )
    d_key, d_value = (
        lax.psum_scatter(
            d_key_terms.reshape(block, local_width).astype(jnp.bfloat16),
            "ctx",
            scatter_dimension=0,
            tiled=True,
        ).astype(jnp.float32),
        lax.psum_scatter(
            d_value_terms.reshape(block, local_width).astype(jnp.bfloat16),
            "ctx",
            scatter_dimension=0,
            tiled=True,
        ).astype(jnp.float32),
    )
    d_query = d_query_acc.reshape(rows, local_width) * 0.125
    g_bqv = jnp.stack([jnp.sum(d_query, axis=0), jnp.sum(d_value, axis=0)])
    d_query_b = d_query.astype(bf)
    d_key_b = d_key.astype(bf)
    d_value_b = d_value.astype(bf)
    g_qkv = jnp.stack(
        [dot32(normed1.T, d_query_b), dot32(normed1.T, d_key_b), dot32(normed1.T, d_value_b)]
    )
    d_local = (
        dot32(d_query_b, wq_back[0].T)
        + dot32(d_key_b, wq_back[1].T)
        + dot32(d_value_b, wq_back[2].T)
    )
    d_normed1 = lax.psum(d_local.astype(jnp.bfloat16), "tp").astype(jnp.float32)
    norm_back1 = jax.vjp(layer_norm, x_f, ln1_gain, ln1_bias)[1]
    d_norm1, g_ln1g, g_ln1b = norm_back1(d_normed1)
    grad_inputs = (d_hidden + d_norm1).astype(bf)
    part_qkv, part_out, part_fc, part_proj = (
        lax.psum_scatter(
            g_qkv.astype(jnp.bfloat16), "shard", scatter_dimension=1, tiled=True
        ).astype(jnp.float32),
        lax.psum_scatter(
            g_out.astype(jnp.bfloat16), "shard", scatter_dimension=1, tiled=True
        ).astype(jnp.float32),
        lax.psum_scatter(
            g_fc.astype(jnp.bfloat16), "shard", scatter_dimension=0, tiled=True
        ).astype(jnp.float32),
        lax.psum_scatter(
            g_proj.astype(jnp.bfloat16), "shard", scatter_dimension=1, tiled=True
        ).astype(jnp.float32),
    )
    sum_qkv, sum_out, sum_fc, sum_proj = (
        lax.psum(part_qkv.astype(jnp.bfloat16), "ctx").astype(jnp.float32),
        lax.psum(part_out.astype(jnp.bfloat16), "ctx").astype(jnp.float32),
        lax.psum(part_fc.astype(jnp.bfloat16), "ctx").astype(jnp.float32),
        lax.psum(part_proj.astype(jnp.bfloat16), "ctx").astype(jnp.float32),
    )
    small = lax.psum(
        (g_bqv, g_bout, g_bfc, g_bproj, g_ln1g, g_ln1b, g_ln2g, g_ln2b), ("shard", "ctx")
    )
    return (
        outputs,
        grad_inputs,
        sum_qkv,
        sum_out,
        sum_fc,
        sum_proj,
        small[0],
        small[1],
        small[2],
        small[3],
        small[4],
        small[5],
        small[6],
        small[7],
    )


MESH = pl.DeviceIdType.MESH
VMEM = pl.BlockSpec(memory_space=pltpu.VMEM)
DMA = pltpu.SemaphoreType.DMA


def signal(peer):
    pl.semaphore_signal(pltpu.get_barrier_semaphore(), inc=1, device_id=peer, device_id_type=MESH)


def await_signals(count):
    pl.semaphore_wait(pltpu.get_barrier_semaphore(), count)


def remote(src, dst, send_sem, recv_sem, peer):
    return pltpu.make_async_remote_copy(
        src_ref=src,
        dst_ref=dst,
        send_sem=send_sem,
        recv_sem=recv_sem,
        device_id=peer,
        device_id_type=MESH,
    )


def comm_call(kernel, out_shape, scratch, ident, *operands, after=()):
    used, unread = len(operands), len(after)

    def body(*refs):
        kernel(*refs[:used], *refs[used + unread :])

    return pl.pallas_call(
        body,
        out_shape=out_shape,
        in_specs=[VMEM] * used + [pl.BlockSpec(memory_space=pl.ANY)] * unread,
        out_specs=[VMEM] * len(out_shape),
        scratch_shapes=scratch,
        compiler_params=pltpu.CompilerParams(collective_id=ident, has_side_effects=True),
        cost_estimate=pl.CostEstimate(flops=0, bytes_accessed=1 << 24, transcendentals=0),
    )(*operands, *after)


class Copies:
    def __init__(self, send_sem, recv_sem):
        self.send_sem, self.recv_sem, self.started = send_sem, recv_sem, []

    def send(self, src, dst, peer):
        at = len(self.started)
        copy = remote(src, dst, self.send_sem.at[at], self.recv_sem.at[at], peer)
        copy.start()
        self.started.append(copy)
        return copy

    def finish(self):
        for copy in self.started:
            copy.wait_send()


def plane_peers():
    s, t = lax.axis_index("shard"), lax.axis_index("tp")
    return s, t, {"tp": 1 - t}, {"shard": s ^ 1}, {"shard": s ^ 2}


def greet_plane():
    s, t, other, along, across = plane_peers()
    for peer in (other, along, across):
        signal(peer)
    await_signals(3)


def plane_gather(arrays, ident, after=()):
    count = lax.axis_size("shard") * 2
    total = len(arrays)
    shapes = [
        jax.ShapeDtypeStruct((a.shape[0], count) + a.shape[1:], a.dtype) for a in arrays
    ]
    sems = 13 * total

    def kernel(*refs):
        ins, outs = refs[:total], refs[total : 2 * total]
        send_sem, recv_sem, own_sem = refs[2 * total :]
        s, t, other, along, across = plane_peers()
        greet_plane()
        copies = Copies(send_sem, recv_sem)
        flights = []
        for a in range(total):
            half = ins[a].shape[0] // 2

            def slot(index, part=None, out=outs[a], half=half):
                if part is None:
                    return out.at[:, index * 2 + t]
                return out.at[pl.ds(part * half, half), index * 2 + t]

            def piece(part, ref=ins[a], half=half):
                return ref.at[pl.ds(part * half, half)]

            own = pltpu.make_async_copy(ins[a], slot(s), own_sem.at[a])
            own.start()
            x0 = copies.send(piece(0), slot(s, 0), along)
            y1 = copies.send(piece(1), slot(s, 1), across)
            x1 = copies.send(piece(1), slot(s, 1), along)
            y0 = copies.send(piece(0), slot(s, 0), across)
            pair = copies.send(ins[a], slot(s), other)
            flights.append((slot, own, x0, y1, x1, y0, pair))
        passed, late = [], []
        for slot, own, x0, y1, x1, y0, pair in flights:
            x0.wait_recv()
            dy = copies.send(slot(s ^ 1, 0), slot(s ^ 1, 0), across)
            passed.append(copies.send(slot(s ^ 1, 0), slot(s ^ 1, 0), other))
            y1.wait_recv()
            dx = copies.send(slot(s ^ 2, 1), slot(s ^ 2, 1), along)
            passed.append(copies.send(slot(s ^ 2, 1), slot(s ^ 2, 1), other))
            late.append((dx, dy))
        for (slot, own, x0, y1, x1, y0, pair), (dx, dy) in zip(flights, late):
            x1.wait_recv()
            passed.append(copies.send(slot(s ^ 1, 1), slot(s ^ 1, 1), other))
            y0.wait_recv()
            passed.append(copies.send(slot(s ^ 2, 0), slot(s ^ 2, 0), other))
            dy.wait_recv()
            passed.append(copies.send(slot(s ^ 3, 0), slot(s ^ 3, 0), other))
            dx.wait_recv()
            passed.append(copies.send(slot(s ^ 3, 1), slot(s ^ 3, 1), other))
            passed.append(pair)
            own.wait()
        for copy in passed:
            copy.wait_recv()
        copies.finish()

    return comm_call(
        kernel, shapes, [DMA((sems,)), DMA((sems,)), DMA((total,))], ident, *arrays, after=after
    )


def plane_scatter(values, ident, after=(), line=()):
    pieces, count, rows, cols = values.shape
    half = pieces // 2
    many = len(line)
    f32 = jnp.float32
    bf = jnp.bfloat16

    def kernel(p_ref, *refs):
        line_in, o_ref, line_out = refs[:many], refs[many], refs[many + 1 : 2 * many + 1]
        line_got = refs[2 * many + 1 : 3 * many + 1]
        got, staged, relayed, arrived, send_sem, recv_sem = refs[3 * many + 1 : 3 * many + 7]
        s, t, other, along, across = plane_peers()
        c = lax.axis_index("ctx")
        for peer in (other, along, across):
            signal(peer)
        steps = (3, 2, 1) if many else ()
        for step in steps:
            signal({"ctx": c ^ step})
        await_signals(3 + len(steps))
        copies = Copies(send_sem, recv_sem)
        low, high = pl.ds(0, half), pl.ds(half, half)
        first = {
            step: copies.send(p_ref.at[:, (s ^ step) * 2 + 1 - t], got.at[step], other)
            for step in (3, 1, 2, 0)
        }

        def both(step):
            first[step].wait_recv()
            return p_ref[:, (s ^ step) * 2 + t].astype(f32) + got[step].astype(f32)

        def line_copy(a, step):
            line_send, line_recv = refs[3 * many + 7 :]
            return remote(
                line_in[a].at[c ^ step],
                line_got[a].at[step - 1],
                line_send.at[a * 3 + step - 1],
                line_recv.at[a * 3 + step - 1],
                {"ctx": c ^ step},
            )

        for a in range(many):
            for step in steps:
                line_copy(a, step).start()
        staged[2] = both(3).astype(bf)
        d0 = copies.send(staged.at[2, low], relayed.at[0], along)
        d1 = copies.send(staged.at[2, high], relayed.at[1], across)
        x_sum = both(1)
        staged[0, low] = x_sum[:half].astype(bf)
        x0 = copies.send(staged.at[0, low], arrived.at[0, low], along)
        y_sum = both(2)
        staged[1, high] = y_sum[half:].astype(bf)
        y1 = copies.send(staged.at[1, high], arrived.at[1, high], across)
        d1.wait_recv()
        staged[0, high] = (x_sum[half:] + relayed[1].astype(f32)).astype(bf)
        x1 = copies.send(staged.at[0, high], arrived.at[0, high], along)
        d0.wait_recv()
        staged[1, low] = (y_sum[:half] + relayed[0].astype(f32)).astype(bf)
        y0 = copies.send(staged.at[1, low], arrived.at[1, low], across)
        o_ref[...] = both(0)
        x0.wait_recv()
        y0.wait_recv()
        o_ref[low] += arrived[0, low].astype(f32) + arrived[1, low].astype(f32)
        x1.wait_recv()
        y1.wait_recv()
        o_ref[high] += arrived[0, high].astype(f32) + arrived[1, high].astype(f32)
        for a in range(many):
            for step in steps:
                line_copy(a, step).wait_recv()
            total = line_in[a][c].astype(f32)
            for step in steps:
                total = total + line_got[a][step - 1].astype(f32)
            line_out[a][...] = total.astype(bf)
        copies.finish()
        for a in range(many):
            for step in steps:
                line_copy(a, step).wait_send()

    outs = comm_call(
        kernel,
        [jax.ShapeDtypeStruct((pieces, rows, cols), f32)]
        + [jax.ShapeDtypeStruct(a.shape[1:], bf) for a in line],
        [pltpu.VMEM((3,) + a.shape[1:], bf) for a in line]
        + [
            pltpu.VMEM((4, pieces, rows, cols), bf),
            pltpu.VMEM((3, pieces, rows, cols), bf),
            pltpu.VMEM((2, half, rows, cols), bf),
            pltpu.VMEM((2, pieces, rows, cols), bf),
            DMA((10,)),
            DMA((10,)),
        ]
        + ([DMA((3 * many,))] * 2 if many else []),
        ident,
        values,
        *line,
        after=after,
    )
    return (outs[0], outs[1:]) if many else outs[0]


def swap_peers():
    s, c = lax.axis_index("shard"), lax.axis_index("ctx")
    return s, c, s == c


def view(ref, axis, index, size):
    start = pl.multiple_of(index * size, size)
    return ref.at[tuple(pl.ds(start, size) if d == axis else slice(None) for d in range(len(ref.shape)))]


def exchange(copies, own_sem, ins, outs, cuts):
    s = lax.axis_index("shard")
    waits = []
    for a, (split, concat) in enumerate(cuts):
        width = ins[a].shape[split] // 4
        depth = ins[a].shape[concat]
        for step in (3, 1, 2):
            waits.append(
                copies.send(
                    view(ins[a], split, s ^ step, width),
                    view(outs[a], concat, s, depth),
                    {"shard": s ^ step},
                ).wait_recv
            )
        own = pltpu.make_async_copy(
            view(ins[a], split, s, width), view(outs[a], concat, s, depth), own_sem.at[a]
        )
        own.start()
        waits.append(own.wait)
    return waits


def exchanged_shapes(arrays, cuts):
    shapes = []
    for array, (split, concat) in zip(arrays, cuts):
        shape = list(array.shape)
        shape[split] //= 4
        shape[concat] *= 4
        shapes.append(jax.ShapeDtypeStruct(tuple(shape), array.dtype))
    return shapes


def all_to_all(arrays, cuts, ident, after=()):
    total = len(arrays)

    def kernel(*refs):
        ins, outs = refs[:total], refs[total : 2 * total]
        send_sem, recv_sem, own_sem = refs[2 * total :]
        s = lax.axis_index("shard")
        for step in (1, 2, 3):
            signal({"shard": s ^ step})
        await_signals(3)
        copies = Copies(send_sem, recv_sem)
        for wait in exchange(copies, own_sem, ins, outs, cuts):
            wait()
        copies.finish()

    sems = total * 3
    return comm_call(
        kernel,
        exchanged_shapes(arrays, cuts),
        [DMA((sems,)), DMA((sems,)), DMA((total,))],
        ident,
        *arrays,
        after=after,
    )


def enter(rows, weights, cuts, ident):
    many, total = len(rows), len(weights)
    shapes = [jax.ShapeDtypeStruct((a.shape[0],) + a.shape[2:], a.dtype) for a in rows]
    shapes += exchanged_shapes(weights, cuts)

    def kernel(*refs):
        ins, outs = refs[: many + total], refs[many + total : 2 * (many + total)]
        row_send, row_recv, send_sem, recv_sem, own_sem = refs[2 * (many + total) :]
        s, c, same = swap_peers()
        t = lax.axis_index("tp")
        for step in range(4):
            def tell(step=step):
                signal({"shard": c, "ctx": c ^ step})

            if step == 0:
                pl.when(jnp.logical_not(same))(tell)
            else:
                tell()
        for step in (1, 2, 3):
            signal({"shard": s ^ step})
        await_signals(jnp.where(same, 6, 7))

        def row_copy(a, step):
            q = s ^ step
            return remote(
                ins[a].at[q, t],
                outs[a].at[c],
                row_send.at[a * 4 + step],
                row_recv.at[a * 4 + c],
                {"shard": q, "ctx": s},
            )

        def kept(a):
            return pltpu.make_async_copy(ins[a].at[s, t], outs[a].at[c], row_recv.at[a * 4 + c])

        for a in range(many):
            for step in (3, 1, 2):
                row_copy(a, step).start()
            pl.when(same)(lambda a=a: kept(a).start())
            pl.when(jnp.logical_not(same))(lambda a=a: row_copy(a, 0).start())
        copies = Copies(send_sem, recv_sem)
        waits = exchange(copies, own_sem, ins[many:], outs[many:], cuts)
        for a in range(many):
            for j in range(4):
                pltpu.make_async_copy(ins[a].at[0, 0], outs[a].at[j], row_recv.at[a * 4 + j]).wait()
        for wait in waits:
            wait()
        for a in range(many):
            for step in (1, 2, 3):
                row_copy(a, step).wait_send()
            pl.when(jnp.logical_not(same))(lambda a=a: row_copy(a, 0).wait_send())
        copies.finish()

    sems = max(total * 3, 1)
    outs = comm_call(
        kernel,
        shapes,
        [DMA((many * 4,)), DMA((many * 4,)), DMA((sems,)), DMA((sems,)), DMA((max(total, 1),))],
        ident,
        *rows,
        *weights,
    )
    return outs[:many], outs[many:]


def leave(rows, small, grad_out, grad_qkv, ident, after=()):
    many = len(rows)
    bf = jnp.bfloat16
    shapes = [jax.ShapeDtypeStruct((4, 2) + a.shape[1:], a.dtype) for a in rows]
    shapes.append(jax.ShapeDtypeStruct(small.shape, small.dtype))
    depth, span = grad_out.shape[0], grad_out.shape[1] // 4
    shapes.append(jax.ShapeDtypeStruct((4, 4, depth, span), bf))
    triple, _, tall, wide = grad_qkv.shape
    shapes.append(jax.ShapeDtypeStruct((triple, 4, tall, 4 * wide), bf))

    def kernel(*refs):
        ins, small_in, out_in, qkv_in = refs[:many], refs[many], refs[many + 1], refs[many + 2]
        refs = refs[many + 3 :]
        outs, small_out, out_all, qkv_all = refs[:many], refs[many], refs[many + 1], refs[many + 2]
        (row_send, row_recv, send_sem, recv_sem, near, line, near_send, near_recv, line_send,
         line_recv, back_send, back_recv, turn_send, turn_recv, own_sem, far_send,
         far_recv) = refs[many + 3 :]
        s, c, same = swap_peers()
        t = lax.axis_index("tp")
        me = s * 2 + t
        other = {"tp": 1 - t}
        plane = [(step, swap) for step in (3, 1, 2, 0) for swap in (0, 1) if step or swap]
        place = lambda step, swap: {"shard": s ^ step, "tp": t ^ swap}
        for step in range(4):
            def tell(step=step):
                signal({"shard": s ^ step, "ctx": s})

            if step == 0:
                pl.when(jnp.logical_not(same))(tell)
            else:
                tell()
        for step, swap in plane:
            signal(place(step, swap))
        for step in (1, 2, 3):
            signal({"ctx": c ^ step})
        await_signals(jnp.where(same, 6, 7) + len(plane))

        def near_copy(i):
            step, swap = plane[i]
            return remote(
                small_in.at[(s ^ step) * 2 + (t ^ swap)],
                near.at[me],
                near_send.at[i],
                near_recv.at[me],
                place(step, swap),
            )

        for i in range(len(plane)):
            near_copy(i).start()

        def out_piece(q):
            return view(out_in, 1, q, span)

        def qkv_slot(line_at, q):
            start = pl.multiple_of(q * wide, wide)
            return qkv_all.at[:, line_at, :, pl.ds(start, wide)]

        def turned(kind, step):
            q = s ^ step
            if kind == 0:
                src, dst = out_piece(q), out_all.at[s, c]
            else:
                src, dst = qkv_in.at[:, q], qkv_slot(c, s)
            at = kind * 3 + step - 1
            return remote(src, dst, turn_send.at[at], turn_recv.at[at], {"shard": q})

        def far(kind, step, hop):
            q = s ^ step
            if kind == 0:
                src, dst = out_all.at[q, c], out_all.at[q, c]
                src = out_piece(s) if step == 0 else src
            else:
                src, dst = qkv_slot(c, q), qkv_slot(c, q)
                src = qkv_in.at[:, s] if step == 0 else src
            at = (kind * 4 + step) * 3 + hop - 1
            return remote(src, dst, far_send.at[at], far_recv.at[at], {"ctx": c ^ hop})

        own = [
            pltpu.make_async_copy(out_piece(s), out_all.at[s, c], own_sem.at[0]),
            pltpu.make_async_copy(qkv_in.at[:, s], qkv_slot(c, s), own_sem.at[1]),
        ]
        for copy in own:
            copy.start()
        for kind in (0, 1):
            for step in (3, 1, 2):
                turned(kind, step).start()

        def row_copy(a, step):
            j = c ^ step
            return remote(
                ins[a].at[j],
                outs[a].at[s, t],
                row_send.at[a * 4 + step],
                row_recv.at[a * 4 + s],
                {"shard": c, "ctx": j},
            )

        def kept(a):
            return pltpu.make_async_copy(ins[a].at[c], outs[a].at[s, t], row_recv.at[a * 4 + s])

        for a in range(many):
            for step in (3, 1, 2):
                row_copy(a, step).start()
            pl.when(same)(lambda a=a: kept(a).start())
            pl.when(jnp.logical_not(same))(lambda a=a: row_copy(a, 0).start())
        for kind in (0, 1):
            for hop in (3, 2, 1):
                far(kind, 0, hop).start()

        def landed(buffer, sem, index):
            pltpu.make_async_copy(small_in.at[0], buffer.at[index], sem.at[index]).wait()

        near[me] = small_in[me]
        for step, swap in plane:
            landed(near, near_recv, (s ^ step) * 2 + (t ^ swap))
        total = near[0]
        for i in range(1, 8):
            total = total + near[i]
        line[c] = total

        def line_copy(step):
            return remote(
                line.at[c], line.at[c], line_send.at[step], line_recv.at[c], {"ctx": c ^ step}
            )

        for step in (1, 2, 3):
            line_copy(step).start()
        for step in (1, 2, 3):
            for kind in (0, 1):
                turned(kind, step).wait_recv()
                for hop in (3, 2, 1):
                    far(kind, step, hop).start()
        for step in (1, 2, 3):
            landed(line, line_recv, c ^ step)
        small_out[me] = line[0] + line[1] + line[2] + line[3]

        def back_copy(i):
            step, swap = plane[i]
            return remote(
                small_out.at[me],
                small_out.at[me],
                back_send.at[i],
                back_recv.at[me],
                place(step, swap),
            )

        for i in range(len(plane)):
            back_copy(i).start()
        copies = Copies(send_sem, recv_sem)
        passed = []
        for a in range(many):
            for step in range(4):
                q = s ^ step
                pltpu.make_async_copy(ins[a].at[0], outs[a].at[q, t], row_recv.at[a * 4 + q]).wait()
                passed.append(copies.send(outs[a].at[q, t], outs[a].at[q, t], other))
        for copy in passed:
            copy.wait_recv()
        for step, swap in plane:
            landed(small_out, back_recv, (s ^ step) * 2 + (t ^ swap))
        for kind in (0, 1):
            for step in range(4):
                for hop in (1, 2, 3):
                    far(kind, step, hop).wait_recv()
        copies.finish()
        for copy in own:
            copy.wait()
        for a in range(many):
            for step in (1, 2, 3):
                row_copy(a, step).wait_send()
            pl.when(jnp.logical_not(same))(lambda a=a: row_copy(a, 0).wait_send())
        for i in range(len(plane)):
            near_copy(i).wait_send()
            back_copy(i).wait_send()
        for step in (1, 2, 3):
            line_copy(step).wait_send()
            for kind in (0, 1):
                turned(kind, step).wait_send()
        for kind in (0, 1):
            for step in range(4):
                for hop in (1, 2, 3):
                    far(kind, step, hop).wait_send()

    shape = small.shape[1:]
    outs = comm_call(
        kernel,
        shapes,
        [
            DMA((many * 4,)),
            DMA((many * 4,)),
            DMA((many * 4,)),
            DMA((many * 4,)),
            pltpu.VMEM((8,) + shape, small.dtype),
            pltpu.VMEM((4,) + shape, small.dtype),
            DMA((7,)),
            DMA((8,)),
            DMA((4,)),
            DMA((4,)),
            DMA((7,)),
            DMA((8,)),
            DMA((6,)),
            DMA((6,)),
            DMA((2,)),
            DMA((24,)),
            DMA((24,)),
        ],
        ident,
        *rows,
        small,
        grad_out,
        grad_qkv,
        after=after,
    )
    return outs[:many], outs[many], outs[many + 1], outs[many + 2]


def norm_back(values, gain, d_out):
    mean = jnp.mean(values, axis=-1, keepdims=True)
    centred = values - mean
    scale = lax.rsqrt(jnp.mean(centred * centred, axis=-1, keepdims=True) + 1e-05)
    unit = centred * scale
    d_unit = d_out * gain
    first = jnp.mean(d_unit, axis=-1, keepdims=True)
    second = jnp.mean(d_unit * unit, axis=-1, keepdims=True)
    d_values = (d_unit - first - unit * second) * scale
    return d_values, jnp.sum(d_out * unit, axis=0), jnp.sum(d_out, axis=0)


def attention(query, key, value, allowed, heads):
    f32 = jnp.float32
    parts = []
    saved = []
    for head in range(heads):
        cols = slice(head * HEAD_DIM, (head + 1) * HEAD_DIM)
        scores = lax.dot_general(
            query[:, cols], key[:, cols], (((1,), (1,)), ((), ())), preferred_element_type=f32
        )
        weights = jnp.where(allowed, jnp.exp(scores), 0.0)
        total = jnp.sum(weights, axis=1, keepdims=True)
        parts.append(dot32(weights.astype(jnp.bfloat16), value[:, cols]) / total)
        saved.append(jnp.log(total))
    return jnp.concatenate(parts, axis=1).astype(jnp.bfloat16), saved


def attention_back(query, key, value, attended, d_attended, allowed, saved, heads):
    f32 = jnp.float32
    bf = jnp.bfloat16
    d_q, d_k, d_v = [], [], []
    for head in range(heads):
        cols = slice(head * HEAD_DIM, (head + 1) * HEAD_DIM)
        q, k, v, da = query[:, cols], key[:, cols], value[:, cols], d_attended[:, cols]
        delta = jnp.sum(da.astype(f32) * attended[:, cols].astype(f32), axis=1, keepdims=True)
        scores = lax.dot_general(q, k, (((1,), (1,)), ((), ())), preferred_element_type=f32)
        probs = jnp.where(allowed, jnp.exp(scores - saved[head]), 0.0)
        d_v.append(
            lax.dot_general(
                probs.astype(bf), da, (((0,), (0,)), ((), ())), preferred_element_type=f32
            )
        )
        d_probs = lax.dot_general(da, v, (((1,), (1,)), ((), ())), preferred_element_type=f32)
        d_scores = (probs * (d_probs - delta)).astype(bf)
        d_q.append(dot32(d_scores, k))
        d_k.append(
            lax.dot_general(d_scores, q, (((0,), (0,)), ((), ())), preferred_element_type=f32)
        )
    join = lambda items: jnp.concatenate(items, axis=1)
    return join(d_q) * 0.125, join(d_k), join(d_v)


def t_dot(left, right):
    return lax.dot_general(left, right, (((0,), (0,)), ((), ())), preferred_element_type=jnp.float32)


def dot_t(left, right):
    return lax.dot_general(left, right, (((1,), (1,)), ((), ())), preferred_element_type=jnp.float32)


def on_device_plane(
    inputs,
    lengths,
    cotangent,
    w_qkv,
    w_out,
    w_fc,
    w_proj,
    b_qv,
    b_out,
    b_fc,
    b_proj,
    ln1_gain,
    ln1_bias,
    ln2_gain,
    ln2_bias,
):
    bf = jnp.bfloat16
    f32 = jnp.float32
    shards = lax.axis_size("shard")
    cores = lax.axis_size("tp")
    s = lax.axis_index("shard")
    t = lax.axis_index("tp")
    model = inputs.shape[1]
    rows = inputs.shape[0] // (shards * cores)
    own = rows * shards
    block = own * shards * cores
    width = b_qv.shape[1] // shards
    heads = width // HEAD_DIM
    units = b_fc.shape[0] // shards
    cut = lambda array: array.reshape(shards, cores, rows, model)
    flat = lambda array: array.reshape(-1, model)
    pieces = lambda array: array.reshape(shards, rows, model)
    spread = lambda array: array.astype(bf).reshape(shards, shards * cores, rows, model)

    pairs = [(a * shards + b, b * shards + a) for a in range(shards) for b in range(shards)]
    lens = lax.ppermute(lengths, ("shard", "ctx"), pairs)[0]
    (x_own, cot_own), (wqkv, wout, wfc, wproj) = enter(
        [cut(inputs), cut(cotangent)],
        [w_qkv, w_out, w_fc, w_proj],
        [(2, 1), (0, 1), (1, 0), (0, 1)],
        1,
    )
    x_f = flat(x_own).astype(f32)
    cot_f = flat(cot_own).astype(f32)
    normed1, cot = [
        flat(array)
        for array in plane_gather(
            [pieces(layer_norm(x_f, ln1_gain, ln1_bias).astype(bf)), cot_own], 2
        )
    ]
    b_qv_own = lax.dynamic_slice_in_dim(b_qv, s * width, width, axis=1)
    b_fc_own = lax.dynamic_slice_in_dim(b_fc, s * units, units, axis=0)

    seg = segment_ids(lens, block)
    places = jnp.arange(block, dtype=jnp.int32)
    allowed = (places[None, :] <= places[:, None]) & (seg[None, :] == seg[:, None])

    query = ((dot32(normed1, wqkv[0]) + b_qv_own[0]) * 0.125).astype(bf)
    key = dot32(normed1, wqkv[1]).astype(bf)
    value = (dot32(normed1, wqkv[2]) + b_qv_own[1]).astype(bf)
    attended, saved = attention(query, key, value, allowed, heads)
    hidden = x_f + flat(plane_scatter(spread(dot32(attended, wout)), 3)) + b_out
    normed2 = flat(
        plane_gather([pieces(layer_norm(hidden, ln2_gain, ln2_bias).astype(bf))], 4)[0]
    )
    pre = dot32(normed2, wfc) + b_fc_own
    act = gelu_tanh(pre).astype(bf)
    d_act = dot_t(cot, wproj)
    d_pre = jax.vjp(gelu_tanh, pre)[1](d_act)[0]
    d_pre_b = d_pre.astype(bf)
    g_proj = t_dot(act, cot).astype(bf).reshape(shards, -1, model)
    g_fc = (
        t_dot(normed2, d_pre_b).astype(bf).reshape(shards, shards, -1, units).transpose(1, 0, 2, 3)
    )
    line_parts = [
        lax.psum_scatter(part, "ctx", scatter_dimension=0, tiled=False) for part in (g_proj, g_fc)
    ]
    d_normed2 = flat(plane_scatter(spread(dot_t(d_pre_b, wfc)), 5))
    g_bfc = jnp.sum(d_pre, axis=0)

    d_norm2, g_ln2g, g_ln2b = norm_back(hidden, ln2_gain, d_normed2)
    d_hidden = cot_f + d_norm2
    d_hidden_b = flat(plane_gather([pieces(d_hidden.astype(bf))], 6)[0])
    mlp_total = flat(plane_scatter(spread(dot32(act, wproj)), 7, (d_hidden_b,)))
    outputs = (hidden + mlp_total + b_proj).astype(bf)
    g_proj_line, g_fc_line = all_to_all(line_parts, [(1, 0), (0, 2)], 8, (mlp_total,))
    g_out = t_dot(attended, d_hidden_b)
    d_attended = dot_t(d_hidden_b, wout).astype(bf)
    d_query, d_key, d_value = attention_back(
        query, key, value, attended, d_attended, allowed, saved, heads
    )
    d_query_b, d_key_b, d_value_b = d_query.astype(bf), d_key.astype(bf), d_value.astype(bf)
    g_qkv = jnp.stack([t_dot(normed1, d_query_b), t_dot(normed1, d_key_b), t_dot(normed1, d_value_b)])
    g_out = g_out.astype(bf).reshape(shards, -1, model)
    g_qkv = g_qkv.astype(bf).reshape(3, shards, shards, -1, width).transpose(2, 0, 1, 3, 4)
    d_normed1, (g_out_line, g_qkv_line) = plane_scatter(
        spread(dot_t(d_query_b, wqkv[0]) + dot_t(d_key_b, wqkv[1]) + dot_t(d_value_b, wqkv[2])),
        9,
        line=(g_out, g_qkv),
    )
    d_normed1 = flat(d_normed1)
    d_norm1, g_ln1g, g_ln1b = norm_back(x_f, ln1_gain, d_normed1)
    grad_inputs = (d_hidden + d_norm1).astype(bf)

    def line_gather(part):
        return lax.all_gather(part, "ctx", axis=0, tiled=False).astype(f32)

    depth = g_proj.shape[1]
    sum_proj = line_gather(g_proj_line.reshape(shards, depth, -1)).transpose(1, 0, 2, 3)
    sum_proj = sum_proj.reshape(shards * units, -1)
    sum_fc = line_gather(g_fc_line.reshape(-1, shards * units)).reshape(-1, shards * units)

    col = t * b_qv.shape[1] + s * width
    g_bqv = jnp.stack([jnp.sum(d_query, axis=0), jnp.sum(d_value, axis=0)])
    full_bqv = lax.dynamic_update_slice(jnp.zeros((2, b_qv.shape[1] * cores), f32), g_bqv, (0, col))
    full_bfc = lax.dynamic_update_slice(
        jnp.zeros((b_fc.shape[0] * cores,), f32), g_bfc, (t * b_fc.shape[0] + s * units,)
    )
    packed = jnp.concatenate(
        [
            full_bqv.reshape(-1),
            full_bfc,
            jnp.sum(d_hidden, axis=0),
            jnp.sum(cot_f, axis=0),
            g_ln1g,
            g_ln1b,
            g_ln2g,
            g_ln2b,
        ]
    )
    filled = packed.size
    tile = shards * cores * 8 * 128
    packed = jnp.pad(packed, (0, -filled % tile)).reshape(shards * cores, -1, 128)
    homes, packed, sum_out, sum_qkv = leave(
        [pieces(outputs), pieces(grad_inputs)], packed, g_out_line, g_qkv_line, 11
    )
    sum_out = sum_out.astype(f32).reshape(shards * width, -1)
    sum_qkv = sum_qkv.astype(f32).reshape(3, -1, shards * width)
    packed = packed.reshape(-1)
    at = full_bqv.size
    sum_bqv = lax.dynamic_slice_in_dim(
        packed[:at].reshape(full_bqv.shape), t * b_qv.shape[1], b_qv.shape[1], axis=1
    )
    sum_bfc = lax.dynamic_slice_in_dim(packed, at + t * b_fc.shape[0], b_fc.shape[0])
    at = at + full_bfc.size
    rest = packed[at : at + 6 * model].reshape(6, model)
    return (
        homes[0].reshape(inputs.shape),
        homes[1].reshape(inputs.shape),
        sum_qkv,
        sum_out,
        sum_fc,
        sum_proj,
        sum_bqv,
        rest[0],
        sum_bfc,
        rest[1],
        rest[2],
        rest[3],
        rest[4],
        rest[5],
    )


def solution(mesh):
    in_specs = (
        P(("shard", "ctx"), None),
        P("shard", None),
        P(("shard", "ctx"), None),
        P(None, "shard", "tp"),
        P("tp", "shard"),
        P("shard", "tp"),
        P("tp", "shard"),
        P(None, "tp"),
        P(),
        P("tp"),
        P(),
        P(),
        P(),
        P(),
        P(),
    )
    out_specs = (
        P(("shard", "ctx"), None),
        P(("shard", "ctx"), None),
        P(None, "shard", "tp"),
        P("tp", "shard"),
        P("shard", "tp"),
        P("tp", "shard"),
        P(None, "tp"),
        P(),
        P("tp"),
        P(),
        P(),
        P(),
        P(),
        P(),
    )
    count = mesh.shape["shard"]
    square = count == mesh.shape["ctx"] and count == 4 and mesh.shape["tp"] == 2
    body = on_device_plane if square else on_device_general
    return jax.shard_map(
        body, mesh=mesh, in_specs=in_specs, out_specs=out_specs, check_vma=False
    )
```

```python
import jax
import jax.numpy as jnp
from jax import lax
from jax.experimental import pallas as pl
from jax.experimental.pallas import tpu as pltpu
from jax.sharding import PartitionSpec as P


HEAD_DIM = 64


def layer_norm(values, gain, shift):
    mean = jnp.mean(values, axis=-1, keepdims=True)
    centred = values - mean
    spread = jnp.mean(centred * centred, axis=-1, keepdims=True)
    return centred * lax.rsqrt(spread + 1e-05) * gain + shift


def gelu_tanh(values):
    return (
        0.5
        * values
        * (1.0 + jnp.tanh(0.7978845608028654 * (values + 0.044715 * values * values * values)))
    )


def segment_ids(lengths, count):
    ends = jnp.cumsum(lengths)
    places = jnp.arange(count, dtype=jnp.int32)
    return jnp.sum((places[:, None] >= ends[None, :]).astype(jnp.int32), axis=1)


def dot32(left, right):
    return jnp.dot(left, right, preferred_element_type=jnp.float32)


def on_device_general(
    inputs,
    lengths,
    cotangent,
    w_qkv,
    w_out,
    w_fc,
    w_proj,
    b_qv,
    b_out,
    b_fc,
    b_proj,
    ln1_gain,
    ln1_bias,
    ln2_gain,
    ln2_bias,
):
    bf = jnp.bfloat16
    f32 = jnp.float32
    rows = inputs.shape[0]
    parts = lax.axis_size("ctx")
    block = rows * parts
    local_width = b_qv.shape[1]
    local_heads = local_width // HEAD_DIM
    seg_all = segment_ids(lengths[0], block)
    first = lax.axis_index("ctx") * rows
    q_pos = first + jnp.arange(rows, dtype=jnp.int32)
    q_seg = lax.dynamic_slice_in_dim(seg_all, first, rows)
    wq_all, wo_all, wfc_all, wproj_all = (
        lax.all_gather(w_qkv, "shard", axis=1, tiled=True),
        lax.all_gather(w_out, "shard", axis=1, tiled=True),
        lax.all_gather(w_fc, "shard", axis=0, tiled=True),
        lax.all_gather(w_proj, "shard", axis=1, tiled=True),
    )
    x_f = inputs.astype(f32)
    normed1 = layer_norm(x_f, ln1_gain, ln1_bias).astype(bf)
    query = ((dot32(normed1, wq_all[0]) + b_qv[0]) * 0.125).astype(bf)
    key = dot32(normed1, wq_all[1]).astype(bf)
    value = (dot32(normed1, wq_all[2]) + b_qv[1]).astype(bf)
    q3 = query.reshape(rows, local_heads, HEAD_DIM)

    def allowed_for(start, count):
        k_pos = start + jnp.arange(count, dtype=jnp.int32)
        k_seg = lax.dynamic_slice_in_dim(seg_all, start, count)
        return (k_pos[None, :] <= q_pos[:, None]) & (k_seg[None, :] == q_seg[:, None])

    k_piece = lax.all_gather(key, "ctx", axis=0, tiled=True)
    v_piece = lax.all_gather(value, "ctx", axis=0, tiled=True)
    count = k_piece.shape[0]
    allowed = allowed_for(jnp.int32(0), count)
    scores = jnp.einsum(
        "rhd,nhd->hrn",
        q3,
        k_piece.reshape(count, local_heads, HEAD_DIM),
        preferred_element_type=f32,
    )
    weights = jnp.where(allowed[None], jnp.exp(scores), 0.0)
    total = jnp.sum(weights, axis=2)
    acc = jnp.einsum(
        "hrn,nhd->hrd",
        weights.astype(bf),
        v_piece.reshape(count, local_heads, HEAD_DIM),
        preferred_element_type=f32,
    )
    total, acc = (total, acc)
    log_total = jnp.log(total)
    attended = (acc / total[:, :, None]).transpose(1, 0, 2).reshape(rows, local_width).astype(bf)
    mixed = lax.psum(dot32(attended, wo_all).astype(jnp.bfloat16), "tp").astype(jnp.float32)
    hidden = x_f + mixed + b_out
    normed2 = layer_norm(hidden, ln2_gain, ln2_bias).astype(bf)
    pre = dot32(normed2, wfc_all) + b_fc
    act = gelu_tanh(pre).astype(bf)
    mlp_total = lax.psum(dot32(act, wproj_all).astype(jnp.bfloat16), "tp").astype(jnp.float32)
    outputs = (hidden + mlp_total + b_proj).astype(bf)
    wq_back, wo_back, wfc_back, wproj_back = (
        lax.all_gather(w_qkv, "shard", axis=1, tiled=True),
        lax.all_gather(w_out, "shard", axis=1, tiled=True),
        lax.all_gather(w_fc, "shard", axis=0, tiled=True),
        lax.all_gather(w_proj, "shard", axis=1, tiled=True),
    )
    grad_f = cotangent.astype(f32)
    g_bproj = jnp.sum(grad_f, axis=0)
    g_proj = dot32(act.T, cotangent)
    d_act = dot32(cotangent, wproj_back.T)
    gelu_back = jax.vjp(gelu_tanh, pre)[1]
    d_pre = gelu_back(d_act)[0]
    g_bfc = jnp.sum(d_pre, axis=0)
    d_pre_b = d_pre.astype(bf)
    g_fc = dot32(normed2.T, d_pre_b)
    d_normed2 = lax.psum(dot32(d_pre_b, wfc_back.T).astype(jnp.bfloat16), "tp").astype(jnp.float32)
    norm_back2 = jax.vjp(layer_norm, hidden, ln2_gain, ln2_bias)[1]
    d_norm2, g_ln2g, g_ln2b = norm_back2(d_normed2)
    d_hidden = grad_f + d_norm2
    g_bout = jnp.sum(d_hidden, axis=0)
    d_hidden_b = d_hidden.astype(bf)
    g_out = dot32(attended.T, d_hidden_b)
    d_attended = dot32(d_hidden_b, wo_back.T).astype(bf)
    da3 = d_attended.reshape(rows, local_heads, HEAD_DIM)
    at3 = attended.reshape(rows, local_heads, HEAD_DIM)
    delta = jnp.einsum("rhd,rhd->hr", da3, at3, preferred_element_type=f32)
    key_all, value_all = (
        lax.all_gather(key, "ctx", axis=0, tiled=True),
        lax.all_gather(value, "ctx", axis=0, tiled=True),
    )
    key_blocks = key_all.reshape(parts, rows, local_heads, HEAD_DIM)
    value_blocks = value_all.reshape(parts, rows, local_heads, HEAD_DIM)
    starts = jnp.arange(parts, dtype=jnp.int32) * rows

    def back_piece(d_query_acc, inputs_piece):
        k_piece, v_piece, start = inputs_piece
        allowed = allowed_for(start, rows)
        scores = jnp.einsum("rhd,nhd->hrn", q3, k_piece, preferred_element_type=f32)
        probs = jnp.where(allowed[None], jnp.exp(scores - log_total[:, :, None]), 0.0)
        d_v = jnp.einsum("hrn,rhd->nhd", probs.astype(bf), da3, preferred_element_type=f32)
        d_probs = jnp.einsum("rhd,nhd->hrn", da3, v_piece, preferred_element_type=f32)
        d_scores_b = (probs * (d_probs - delta[:, :, None])).astype(bf)
        d_query_acc = d_query_acc + jnp.einsum(
            "hrn,nhd->rhd", d_scores_b, k_piece, preferred_element_type=f32
        )
        d_k = jnp.einsum("hrn,rhd->nhd", d_scores_b, q3, preferred_element_type=f32)
        return (d_query_acc, (d_k.reshape(rows, local_width), d_v.reshape(rows, local_width)))

    zero_query = jnp.zeros((rows, local_heads, HEAD_DIM), f32)
    d_query_acc, (d_key_terms, d_value_terms) = lax.scan(
        back_piece, zero_query, (key_blocks, value_blocks, starts)
    )
    d_key, d_value = (
        lax.psum_scatter(
            d_key_terms.reshape(block, local_width).astype(jnp.bfloat16),
            "ctx",
            scatter_dimension=0,
            tiled=True,
        ).astype(jnp.float32),
        lax.psum_scatter(
            d_value_terms.reshape(block, local_width).astype(jnp.bfloat16),
            "ctx",
            scatter_dimension=0,
            tiled=True,
        ).astype(jnp.float32),
    )
    d_query = d_query_acc.reshape(rows, local_width) * 0.125
    g_bqv = jnp.stack([jnp.sum(d_query, axis=0), jnp.sum(d_value, axis=0)])
    d_query_b = d_query.astype(bf)
    d_key_b = d_key.astype(bf)
    d_value_b = d_value.astype(bf)
    g_qkv = jnp.stack(
        [dot32(normed1.T, d_query_b), dot32(normed1.T, d_key_b), dot32(normed1.T, d_value_b)]
    )
    d_local = (
        dot32(d_query_b, wq_back[0].T)
        + dot32(d_key_b, wq_back[1].T)
        + dot32(d_value_b, wq_back[2].T)
    )
    d_normed1 = lax.psum(d_local.astype(jnp.bfloat16), "tp").astype(jnp.float32)
    norm_back1 = jax.vjp(layer_norm, x_f, ln1_gain, ln1_bias)[1]
    d_norm1, g_ln1g, g_ln1b = norm_back1(d_normed1)
    grad_inputs = (d_hidden + d_norm1).astype(bf)
    part_qkv, part_out, part_fc, part_proj = (
        lax.psum_scatter(
            g_qkv.astype(jnp.bfloat16), "shard", scatter_dimension=1, tiled=True
        ).astype(jnp.float32),
        lax.psum_scatter(
            g_out.astype(jnp.bfloat16), "shard", scatter_dimension=1, tiled=True
        ).astype(jnp.float32),
        lax.psum_scatter(
            g_fc.astype(jnp.bfloat16), "shard", scatter_dimension=0, tiled=True
        ).astype(jnp.float32),
        lax.psum_scatter(
            g_proj.astype(jnp.bfloat16), "shard", scatter_dimension=1, tiled=True
        ).astype(jnp.float32),
    )
    sum_qkv, sum_out, sum_fc, sum_proj = (
        lax.psum(part_qkv.astype(jnp.bfloat16), "ctx").astype(jnp.float32),
        lax.psum(part_out.astype(jnp.bfloat16), "ctx").astype(jnp.float32),
        lax.psum(part_fc.astype(jnp.bfloat16), "ctx").astype(jnp.float32),
        lax.psum(part_proj.astype(jnp.bfloat16), "ctx").astype(jnp.float32),
    )
    small = lax.psum(
        (g_bqv, g_bout, g_bfc, g_bproj, g_ln1g, g_ln1b, g_ln2g, g_ln2b), ("shard", "ctx")
    )
    return (
        outputs,
        grad_inputs,
        sum_qkv,
        sum_out,
        sum_fc,
        sum_proj,
        small[0],
        small[1],
        small[2],
        small[3],
        small[4],
        small[5],
        small[6],
        small[7],
    )


MESH = pl.DeviceIdType.MESH
VMEM = pl.BlockSpec(memory_space=pltpu.VMEM)
DMA = pltpu.SemaphoreType.DMA


def signal(peer):
    pl.semaphore_signal(pltpu.get_barrier_semaphore(), inc=1, device_id=peer, device_id_type=MESH)


def await_signals(count):
    pl.semaphore_wait(pltpu.get_barrier_semaphore(), count)


def remote(src, dst, send_sem, recv_sem, peer):
    return pltpu.make_async_remote_copy(
        src_ref=src,
        dst_ref=dst,
        send_sem=send_sem,
        recv_sem=recv_sem,
        device_id=peer,
        device_id_type=MESH,
    )


def comm_call(kernel, out_shape, scratch, ident, *operands, after=()):
    used, unread = len(operands), len(after)

    def body(*refs):
        kernel(*refs[:used], *refs[used + unread :])

    return pl.pallas_call(
        body,
        out_shape=out_shape,
        in_specs=[VMEM] * used + [pl.BlockSpec(memory_space=pl.ANY)] * unread,
        out_specs=[VMEM] * len(out_shape),
        scratch_shapes=scratch,
        compiler_params=pltpu.CompilerParams(collective_id=ident, has_side_effects=True),
        cost_estimate=pl.CostEstimate(flops=0, bytes_accessed=1 << 24, transcendentals=0),
    )(*operands, *after)


class Copies:
    def __init__(self, send_sem, recv_sem):
        self.send_sem, self.recv_sem, self.started = send_sem, recv_sem, []

    def send(self, src, dst, peer):
        at = len(self.started)
        copy = remote(src, dst, self.send_sem.at[at], self.recv_sem.at[at], peer)
        copy.start()
        self.started.append(copy)
        return copy

    def finish(self):
        for copy in self.started:
            copy.wait_send()


def plane_peers():
    s, t = lax.axis_index("shard"), lax.axis_index("tp")
    return s, t, {"tp": 1 - t}, {"shard": s ^ 1}, {"shard": s ^ 2}


def greet_plane(diagonal=0, line=()):
    s, _, other, along, across = plane_peers()
    c = lax.axis_index("ctx")
    peers = [other, along, across]
    if diagonal:
        peers.append({"shard": s ^ 3})
    for step in line:
        peers.append({"ctx": c ^ step})
    for peer in peers:
        signal(peer)
    await_signals(len(peers))


def plane_gather(arrays, ident, after=(), turn=(), cuts=()):
    moved = len(turn)
    count = lax.axis_size("shard") * 2
    total = len(arrays)
    shapes = [
        jax.ShapeDtypeStruct((a.shape[0], count) + a.shape[1:], a.dtype) for a in arrays
    ]
    shapes += exchanged_shapes(turn, cuts)
    every = total + moved
    sems = 13 * total + 3 * moved

    def kernel(*refs):
        ins, outs = refs[:total], refs[every : every + total]
        turn_in, turn_out = refs[total:every], refs[every + total : 2 * every]
        send_sem, recv_sem, own_sem = refs[2 * every :]
        s, t, other, along, across = plane_peers()
        greet_plane(moved)
        copies = Copies(send_sem, recv_sem)
        flights = []
        for a in range(total):
            half = ins[a].shape[0] // 2

            def slot(index, part=None, out=outs[a], half=half):
                if part is None:
                    return out.at[:, index * 2 + t]
                return out.at[pl.ds(part * half, half), index * 2 + t]

            def piece(part, ref=ins[a], half=half):
                return ref.at[pl.ds(part * half, half)]

            own = pltpu.make_async_copy(ins[a], slot(s), own_sem.at[a])
            own.start()
            x0 = copies.send(piece(0), slot(s, 0), along)
            y1 = copies.send(piece(1), slot(s, 1), across)
            x1 = copies.send(piece(1), slot(s, 1), along)
            y0 = copies.send(piece(0), slot(s, 0), across)
            pair = copies.send(ins[a], slot(s), other)
            flights.append((slot, own, x0, y1, x1, y0, pair))
        waits = exchange(copies, own_sem, turn_in, turn_out, cuts, total)
        passed, late = [], []
        for slot, own, x0, y1, x1, y0, pair in flights:
            x0.wait_recv()
            dy = copies.send(slot(s ^ 1, 0), slot(s ^ 1, 0), across)
            passed.append(copies.send(slot(s ^ 1, 0), slot(s ^ 1, 0), other))
            y1.wait_recv()
            dx = copies.send(slot(s ^ 2, 1), slot(s ^ 2, 1), along)
            passed.append(copies.send(slot(s ^ 2, 1), slot(s ^ 2, 1), other))
            late.append((dx, dy))
        for (slot, own, x0, y1, x1, y0, pair), (dx, dy) in zip(flights, late):
            x1.wait_recv()
            passed.append(copies.send(slot(s ^ 1, 1), slot(s ^ 1, 1), other))
            y0.wait_recv()
            passed.append(copies.send(slot(s ^ 2, 0), slot(s ^ 2, 0), other))
            dy.wait_recv()
            passed.append(copies.send(slot(s ^ 3, 0), slot(s ^ 3, 0), other))
            dx.wait_recv()
            passed.append(copies.send(slot(s ^ 3, 1), slot(s ^ 3, 1), other))
            passed.append(pair)
            own.wait()
        for copy in passed:
            copy.wait_recv()
        for wait in waits:
            wait()
        copies.finish()

    return comm_call(
        kernel,
        shapes,
        [DMA((sems,)), DMA((sems,)), DMA((every,))],
        ident,
        *arrays,
        *turn,
        after=after,
    )


def plane_scatter(values, ident, after=(), line=(), turn=(), cuts=()):
    moved = len(turn)
    pieces, _, rows, cols = values.shape
    half = pieces // 2
    many = len(line)
    f32 = jnp.float32
    bf = jnp.bfloat16

    def kernel(p_ref, *refs):
        line_in, turn_in, refs = refs[:many], refs[many : many + moved], refs[many + moved :]
        o_ref, line_out, turn_out = refs[0], refs[1 : many + 1], refs[many + 1 : many + 1 + moved]
        refs = refs[many + 1 + moved :]
        line_got = refs[:many]
        got, staged, relayed, arrived, send_sem, recv_sem, own_sem = refs[many : many + 7]
        s, t, other, along, across = plane_peers()
        c = lax.axis_index("ctx")
        steps = (3, 2, 1) if many else ()
        greet_plane(moved, steps)
        copies = Copies(send_sem, recv_sem)
        low, high = pl.ds(0, half), pl.ds(half, half)
        first = {
            step: copies.send(p_ref.at[:, (s ^ step) * 2 + 1 - t], got.at[step], other)
            for step in (3, 1, 2, 0)
        }

        def both(step):
            first[step].wait_recv()
            return p_ref[:, (s ^ step) * 2 + t].astype(f32) + got[step].astype(f32)

        def line_copy(a, step):
            line_send, line_recv = refs[many + 7 :]
            return remote(
                line_in[a].at[c ^ step],
                line_got[a].at[step - 1],
                line_send.at[a * 3 + step - 1],
                line_recv.at[a * 3 + step - 1],
                {"ctx": c ^ step},
            )

        for a in range(many):
            for step in steps:
                line_copy(a, step).start()
        staged[2] = both(3).astype(bf)
        d0 = copies.send(staged.at[2, low], relayed.at[0], along)
        d1 = copies.send(staged.at[2, high], relayed.at[1], across)
        waits = exchange(copies, own_sem, turn_in, turn_out, cuts)
        x_sum = both(1)
        staged[0, low] = x_sum[:half].astype(bf)
        x0 = copies.send(staged.at[0, low], arrived.at[0, low], along)
        y_sum = both(2)
        staged[1, high] = y_sum[half:].astype(bf)
        y1 = copies.send(staged.at[1, high], arrived.at[1, high], across)
        d1.wait_recv()
        staged[0, high] = (x_sum[half:] + relayed[1].astype(f32)).astype(bf)
        x1 = copies.send(staged.at[0, high], arrived.at[0, high], along)
        d0.wait_recv()
        staged[1, low] = (y_sum[:half] + relayed[0].astype(f32)).astype(bf)
        y0 = copies.send(staged.at[1, low], arrived.at[1, low], across)
        o_ref[...] = both(0)
        x0.wait_recv()
        y0.wait_recv()
        o_ref[low] += arrived[0, low].astype(f32) + arrived[1, low].astype(f32)
        x1.wait_recv()
        y1.wait_recv()
        o_ref[high] += arrived[0, high].astype(f32) + arrived[1, high].astype(f32)
        for a in range(many):
            for step in steps:
                line_copy(a, step).wait_recv()
            total = line_in[a][c].astype(f32)
            for step in steps:
                total = total + line_got[a][step - 1].astype(f32)
            line_out[a][...] = total.astype(bf)
        for wait in waits:
            wait()
        copies.finish()
        for a in range(many):
            for step in steps:
                line_copy(a, step).wait_send()

    outs = comm_call(
        kernel,
        [jax.ShapeDtypeStruct((pieces, rows, cols), f32)]
        + [jax.ShapeDtypeStruct(a.shape[1:], bf) for a in line]
        + exchanged_shapes(turn, cuts),
        [pltpu.VMEM((3,) + a.shape[1:], bf) for a in line]
        + [
            pltpu.VMEM((4, pieces, rows, cols), bf),
            pltpu.VMEM((3, pieces, rows, cols), bf),
            pltpu.VMEM((2, half, rows, cols), bf),
            pltpu.VMEM((2, pieces, rows, cols), bf),
            DMA((10 + 3 * moved,)),
            DMA((10 + 3 * moved,)),
            DMA((max(moved, 1),)),
        ]
        + ([DMA((3 * many,))] * 2 if many else []),
        ident,
        values,
        *line,
        *turn,
        after=after,
    )
    return (outs[0], outs[1:]) if many or moved else outs[0]


def swap_peers():
    s, c = lax.axis_index("shard"), lax.axis_index("ctx")
    return s, c, s == c


def view(ref, axis, index, size):
    start = pl.multiple_of(index * size, size)
    return ref.at[tuple(pl.ds(start, size) if d == axis else slice(None) for d in range(len(ref.shape)))]


def exchange(copies, own_sem, ins, outs, cuts, first=0):
    s = lax.axis_index("shard")
    waits = []
    for a, (split, concat) in enumerate(cuts):
        width = ins[a].shape[split] // 4
        depth = ins[a].shape[concat]
        for step in (3, 1, 2):
            waits.append(
                copies.send(
                    view(ins[a], split, s ^ step, width),
                    view(outs[a], concat, s, depth),
                    {"shard": s ^ step},
                ).wait_recv
            )
        own = pltpu.make_async_copy(
            view(ins[a], split, s, width), view(outs[a], concat, s, depth), own_sem.at[first + a]
        )
        own.start()
        waits.append(own.wait)
    return waits


def exchanged_shapes(arrays, cuts):
    shapes = []
    for array, (split, concat) in zip(arrays, cuts):
        shape = list(array.shape)
        shape[split] //= 4
        shape[concat] *= 4
        shapes.append(jax.ShapeDtypeStruct(tuple(shape), array.dtype))
    return shapes


def enter(rows, weights, cuts, ident):
    many, total = len(rows), len(weights)
    shapes = [jax.ShapeDtypeStruct((a.shape[0],) + a.shape[2:], a.dtype) for a in rows]
    shapes += exchanged_shapes(weights, cuts)

    def kernel(*refs):
        ins, outs = refs[: many + total], refs[many + total : 2 * (many + total)]
        row_send, row_recv, send_sem, recv_sem, own_sem = refs[2 * (many + total) :]
        s, c, same = swap_peers()
        t = lax.axis_index("tp")
        for step in range(4):
            def tell(step=step):
                signal({"shard": c, "ctx": c ^ step})

            if step == 0:
                pl.when(jnp.logical_not(same))(tell)
            else:
                tell()
        for step in (1, 2, 3):
            signal({"shard": s ^ step})
        await_signals(jnp.where(same, 6, 7))

        def row_copy(a, step):
            q = s ^ step
            return remote(
                ins[a].at[q, t],
                outs[a].at[c],
                row_send.at[a * 4 + step],
                row_recv.at[a * 4 + c],
                {"shard": q, "ctx": s},
            )

        def kept(a):
            return pltpu.make_async_copy(ins[a].at[s, t], outs[a].at[c], row_recv.at[a * 4 + c])

        for a in range(many):
            for step in (3, 1, 2):
                row_copy(a, step).start()
            pl.when(same)(lambda a=a: kept(a).start())
            pl.when(jnp.logical_not(same))(lambda a=a: row_copy(a, 0).start())
        copies = Copies(send_sem, recv_sem)
        waits = exchange(copies, own_sem, ins[many:], outs[many:], cuts)
        for a in range(many):
            for j in range(4):
                pltpu.make_async_copy(ins[a].at[0, 0], outs[a].at[j], row_recv.at[a * 4 + j]).wait()
        for wait in waits:
            wait()
        for a in range(many):
            for step in (1, 2, 3):
                row_copy(a, step).wait_send()
            pl.when(jnp.logical_not(same))(lambda a=a: row_copy(a, 0).wait_send())
        copies.finish()

    sems = max(total * 3, 1)
    outs = comm_call(
        kernel,
        shapes,
        [DMA((many * 4,)), DMA((many * 4,)), DMA((sems,)), DMA((sems,)), DMA((max(total, 1),))],
        ident,
        *rows,
        *weights,
    )
    return outs[:many], outs[many:]


def leave(rows, small, grad_out, grad_qkv, ident, after=()):
    many = len(rows)
    bf = jnp.bfloat16
    shapes = [jax.ShapeDtypeStruct((4, 2) + a.shape[1:], a.dtype) for a in rows]
    shapes.append(jax.ShapeDtypeStruct(small.shape, small.dtype))
    depth, span = grad_out.shape[0], grad_out.shape[1] // 4
    shapes.append(jax.ShapeDtypeStruct((4, 4, depth, span), bf))
    triple, _, tall, wide = grad_qkv.shape
    shapes.append(jax.ShapeDtypeStruct((triple, 4, tall, 4 * wide), bf))

    def kernel(*refs):
        ins, small_in, out_in, qkv_in = refs[:many], refs[many], refs[many + 1], refs[many + 2]
        refs = refs[many + 3 :]
        outs, small_out, out_all, qkv_all = refs[:many], refs[many], refs[many + 1], refs[many + 2]
        (row_send, row_recv, send_sem, recv_sem, near, line, near_send, near_recv, line_send,
         line_recv, back_send, back_recv, turn_send, turn_recv, own_sem, far_send,
         far_recv) = refs[many + 3 :]
        s, c, same = swap_peers()
        t = lax.axis_index("tp")
        me = s * 2 + t
        other = {"tp": 1 - t}
        plane = [(step, swap) for step in (3, 1, 2, 0) for swap in (0, 1) if step or swap]
        place = lambda step, swap: {"shard": s ^ step, "tp": t ^ swap}
        for step in range(4):
            def tell(step=step):
                signal({"shard": s ^ step, "ctx": s})

            if step == 0:
                pl.when(jnp.logical_not(same))(tell)
            else:
                tell()
        for step, swap in plane:
            signal(place(step, swap))
        for step in (1, 2, 3):
            signal({"ctx": c ^ step})
        await_signals(jnp.where(same, 6, 7) + len(plane))

        def near_copy(i):
            step, swap = plane[i]
            return remote(
                small_in.at[(s ^ step) * 2 + (t ^ swap)],
                near.at[me],
                near_send.at[i],
                near_recv.at[me],
                place(step, swap),
            )

        for i in range(len(plane)):
            near_copy(i).start()

        def out_piece(q):
            return view(out_in, 1, q, span)

        def qkv_slot(line_at, q):
            start = pl.multiple_of(q * wide, wide)
            return qkv_all.at[:, line_at, :, pl.ds(start, wide)]

        def turned(kind, step):
            q = s ^ step
            if kind == 0:
                src, dst = out_piece(q), out_all.at[s, c]
            else:
                src, dst = qkv_in.at[:, q], qkv_slot(c, s)
            at = kind * 3 + step - 1
            return remote(src, dst, turn_send.at[at], turn_recv.at[at], {"shard": q})

        def far(kind, step, hop):
            q = s ^ step
            if kind == 0:
                src, dst = out_all.at[q, c], out_all.at[q, c]
                src = out_piece(s) if step == 0 else src
            else:
                src, dst = qkv_slot(c, q), qkv_slot(c, q)
                src = qkv_in.at[:, s] if step == 0 else src
            at = (kind * 4 + step) * 3 + hop - 1
            return remote(src, dst, far_send.at[at], far_recv.at[at], {"ctx": c ^ hop})

        own = [
            pltpu.make_async_copy(out_piece(s), out_all.at[s, c], own_sem.at[0]),
            pltpu.make_async_copy(qkv_in.at[:, s], qkv_slot(c, s), own_sem.at[1]),
        ]
        for copy in own:
            copy.start()
        for kind in (0, 1):
            for step in (3, 1, 2):
                turned(kind, step).start()

        def row_copy(a, step):
            j = c ^ step
            return remote(
                ins[a].at[j],
                outs[a].at[s, t],
                row_send.at[a * 4 + step],
                row_recv.at[a * 4 + s],
                {"shard": c, "ctx": j},
            )

        def kept(a):
            return pltpu.make_async_copy(ins[a].at[c], outs[a].at[s, t], row_recv.at[a * 4 + s])

        for a in range(many):
            for step in (3, 1, 2):
                row_copy(a, step).start()
            pl.when(same)(lambda a=a: kept(a).start())
            pl.when(jnp.logical_not(same))(lambda a=a: row_copy(a, 0).start())
        for kind in (0, 1):
            for hop in (3, 2, 1):
                far(kind, 0, hop).start()

        def landed(buffer, sem, index):
            pltpu.make_async_copy(small_in.at[0], buffer.at[index], sem.at[index]).wait()

        near[me] = small_in[me]
        for step, swap in plane:
            landed(near, near_recv, (s ^ step) * 2 + (t ^ swap))
        total = near[0]
        for i in range(1, 8):
            total = total + near[i]
        line[c] = total

        def line_copy(step):
            return remote(
                line.at[c], line.at[c], line_send.at[step], line_recv.at[c], {"ctx": c ^ step}
            )

        for step in (1, 2, 3):
            line_copy(step).start()
        for step in (1, 2, 3):
            for kind in (0, 1):
                turned(kind, step).wait_recv()
                for hop in (3, 2, 1):
                    far(kind, step, hop).start()
        for step in (1, 2, 3):
            landed(line, line_recv, c ^ step)
        small_out[me] = line[0] + line[1] + line[2] + line[3]

        def back_copy(i):
            step, swap = plane[i]
            return remote(
                small_out.at[me],
                small_out.at[me],
                back_send.at[i],
                back_recv.at[me],
                place(step, swap),
            )

        for i in range(len(plane)):
            back_copy(i).start()
        copies = Copies(send_sem, recv_sem)
        passed = []
        for a in range(many):
            for step in range(4):
                q = s ^ step
                pltpu.make_async_copy(ins[a].at[0], outs[a].at[q, t], row_recv.at[a * 4 + q]).wait()
                passed.append(copies.send(outs[a].at[q, t], outs[a].at[q, t], other))
        for copy in passed:
            copy.wait_recv()
        for step, swap in plane:
            landed(small_out, back_recv, (s ^ step) * 2 + (t ^ swap))
        for kind in (0, 1):
            for step in range(4):
                for hop in (1, 2, 3):
                    far(kind, step, hop).wait_recv()
        copies.finish()
        for copy in own:
            copy.wait()
        for a in range(many):
            for step in (1, 2, 3):
                row_copy(a, step).wait_send()
            pl.when(jnp.logical_not(same))(lambda a=a: row_copy(a, 0).wait_send())
        for i in range(len(plane)):
            near_copy(i).wait_send()
            back_copy(i).wait_send()
        for step in (1, 2, 3):
            line_copy(step).wait_send()
            for kind in (0, 1):
                turned(kind, step).wait_send()
        for kind in (0, 1):
            for step in range(4):
                for hop in (1, 2, 3):
                    far(kind, step, hop).wait_send()

    shape = small.shape[1:]
    outs = comm_call(
        kernel,
        shapes,
        [
            DMA((many * 4,)),
            DMA((many * 4,)),
            DMA((many * 4,)),
            DMA((many * 4,)),
            pltpu.VMEM((8,) + shape, small.dtype),
            pltpu.VMEM((4,) + shape, small.dtype),
            DMA((7,)),
            DMA((8,)),
            DMA((4,)),
            DMA((4,)),
            DMA((7,)),
            DMA((8,)),
            DMA((6,)),
            DMA((6,)),
            DMA((2,)),
            DMA((24,)),
            DMA((24,)),
        ],
        ident,
        *rows,
        small,
        grad_out,
        grad_qkv,
        after=after,
    )
    return outs[:many], outs[many], outs[many + 1], outs[many + 2]


def norm_back(values, gain, d_out):
    mean = jnp.mean(values, axis=-1, keepdims=True)
    centred = values - mean
    scale = lax.rsqrt(jnp.mean(centred * centred, axis=-1, keepdims=True) + 1e-05)
    unit = centred * scale
    d_unit = d_out * gain
    first = jnp.mean(d_unit, axis=-1, keepdims=True)
    second = jnp.mean(d_unit * unit, axis=-1, keepdims=True)
    d_values = (d_unit - first - unit * second) * scale
    return d_values, jnp.sum(d_out * unit, axis=0), jnp.sum(d_out, axis=0)


def attention(query, key, value, allowed, heads):
    f32 = jnp.float32
    parts = []
    saved = []
    for head in range(heads):
        cols = slice(head * HEAD_DIM, (head + 1) * HEAD_DIM)
        scores = lax.dot_general(
            query[:, cols], key[:, cols], (((1,), (1,)), ((), ())), preferred_element_type=f32
        )
        weights = jnp.where(allowed, jnp.exp(scores), 0.0)
        total = jnp.sum(weights, axis=1, keepdims=True)
        parts.append(dot32(weights.astype(jnp.bfloat16), value[:, cols]) / total)
        saved.append(jnp.log(total))
    return jnp.concatenate(parts, axis=1).astype(jnp.bfloat16), saved


def attention_back(query, key, value, attended, d_attended, allowed, saved, heads):
    f32 = jnp.float32
    bf = jnp.bfloat16
    d_q, d_k, d_v = [], [], []
    for head in range(heads):
        cols = slice(head * HEAD_DIM, (head + 1) * HEAD_DIM)
        q, k, v, da = query[:, cols], key[:, cols], value[:, cols], d_attended[:, cols]
        delta = jnp.sum(da.astype(f32) * attended[:, cols].astype(f32), axis=1, keepdims=True)
        scores = lax.dot_general(q, k, (((1,), (1,)), ((), ())), preferred_element_type=f32)
        probs = jnp.where(allowed, jnp.exp(scores - saved[head]), 0.0)
        d_v.append(
            lax.dot_general(
                probs.astype(bf), da, (((0,), (0,)), ((), ())), preferred_element_type=f32
            )
        )
        d_probs = lax.dot_general(da, v, (((1,), (1,)), ((), ())), preferred_element_type=f32)
        d_scores = (probs * (d_probs - delta)).astype(bf)
        d_q.append(dot32(d_scores, k))
        d_k.append(
            lax.dot_general(d_scores, q, (((0,), (0,)), ((), ())), preferred_element_type=f32)
        )
    join = lambda items: jnp.concatenate(items, axis=1)
    return join(d_q) * 0.125, join(d_k), join(d_v)


def t_dot(left, right):
    return lax.dot_general(left, right, (((0,), (0,)), ((), ())), preferred_element_type=jnp.float32)


def dot_t(left, right):
    return lax.dot_general(left, right, (((1,), (1,)), ((), ())), preferred_element_type=jnp.float32)


def on_device_plane(
    inputs,
    lengths,
    cotangent,
    w_qkv,
    w_out,
    w_fc,
    w_proj,
    b_qv,
    b_out,
    b_fc,
    b_proj,
    ln1_gain,
    ln1_bias,
    ln2_gain,
    ln2_bias,
):
    bf = jnp.bfloat16
    f32 = jnp.float32
    shards = lax.axis_size("shard")
    cores = lax.axis_size("tp")
    s = lax.axis_index("shard")
    t = lax.axis_index("tp")
    model = inputs.shape[1]
    rows = inputs.shape[0] // (shards * cores)
    own = rows * shards
    block = own * shards * cores
    width = b_qv.shape[1] // shards
    heads = width // HEAD_DIM
    units = b_fc.shape[0] // shards
    cut = lambda array: array.reshape(shards, cores, rows, model)
    flat = lambda array: array.reshape(-1, model)
    pieces = lambda array: array.reshape(shards, rows, model)
    spread = lambda array: array.astype(bf).reshape(shards, shards * cores, rows, model)

    pairs = [(a * shards + b, b * shards + a) for a in range(shards) for b in range(shards)]
    lens = lax.ppermute(lengths, ("shard", "ctx"), pairs)[0]
    (x_own, cot_own), (wqkv, wout, wfc, wproj) = enter(
        [cut(inputs), cut(cotangent)],
        [w_qkv, w_out, w_fc, w_proj],
        [(2, 1), (0, 1), (1, 0), (0, 1)],
        1,
    )
    x_f = flat(x_own).astype(f32)
    cot_f = flat(cot_own).astype(f32)
    normed1, cot = [
        flat(array)
        for array in plane_gather(
            [pieces(layer_norm(x_f, ln1_gain, ln1_bias).astype(bf)), cot_own], 2
        )
    ]
    b_qv_own = lax.dynamic_slice_in_dim(b_qv, s * width, width, axis=1)
    b_fc_own = lax.dynamic_slice_in_dim(b_fc, s * units, units, axis=0)

    seg = segment_ids(lens, block)
    places = jnp.arange(block, dtype=jnp.int32)
    allowed = (places[None, :] <= places[:, None]) & (seg[None, :] == seg[:, None])

    query = ((dot32(normed1, wqkv[0]) + b_qv_own[0]) * 0.125).astype(bf)
    key = dot32(normed1, wqkv[1]).astype(bf)
    value = (dot32(normed1, wqkv[2]) + b_qv_own[1]).astype(bf)
    attended, saved = attention(query, key, value, allowed, heads)
    hidden = x_f + flat(plane_scatter(spread(dot32(attended, wout)), 3)) + b_out
    normed2 = flat(
        plane_gather([pieces(layer_norm(hidden, ln2_gain, ln2_bias).astype(bf))], 4)[0]
    )
    pre = dot32(normed2, wfc) + b_fc_own
    act = gelu_tanh(pre).astype(bf)
    d_act = dot_t(cot, wproj)
    d_pre = jax.vjp(gelu_tanh, pre)[1](d_act)[0]
    d_pre_b = d_pre.astype(bf)
    g_proj = t_dot(act, cot).astype(bf).reshape(shards, -1, model)
    g_fc = (
        t_dot(normed2, d_pre_b).astype(bf).reshape(shards, shards, -1, units).transpose(1, 0, 2, 3)
    )
    line_parts = [
        lax.psum_scatter(part, "ctx", scatter_dimension=0, tiled=False) for part in (g_proj, g_fc)
    ]
    d_normed2 = flat(plane_scatter(spread(dot_t(d_pre_b, wfc)), 5))
    g_bfc = jnp.sum(d_pre, axis=0)

    d_norm2, g_ln2g, g_ln2b = norm_back(hidden, ln2_gain, d_normed2)
    d_hidden = cot_f + d_norm2
    d_hidden_b, g_proj_line = plane_gather(
        [pieces(d_hidden.astype(bf))], 6, turn=line_parts[:1], cuts=[(1, 0)]
    )
    d_hidden_b = flat(d_hidden_b)
    mlp_total, (g_fc_line,) = plane_scatter(
        spread(dot32(act, wproj)), 7, (d_hidden_b,), turn=line_parts[1:], cuts=[(0, 2)]
    )
    mlp_total = flat(mlp_total)
    outputs = (hidden + mlp_total + b_proj).astype(bf)
    g_out = t_dot(attended, d_hidden_b)
    d_attended = dot_t(d_hidden_b, wout).astype(bf)
    d_query, d_key, d_value = attention_back(
        query, key, value, attended, d_attended, allowed, saved, heads
    )
    d_query_b, d_key_b, d_value_b = d_query.astype(bf), d_key.astype(bf), d_value.astype(bf)
    g_qkv = jnp.stack([t_dot(normed1, d_query_b), t_dot(normed1, d_key_b), t_dot(normed1, d_value_b)])
    g_out = g_out.astype(bf).reshape(shards, -1, model)
    g_qkv = g_qkv.astype(bf).reshape(3, shards, shards, -1, width).transpose(2, 0, 1, 3, 4)
    d_normed1, (g_out_line, g_qkv_line) = plane_scatter(
        spread(dot_t(d_query_b, wqkv[0]) + dot_t(d_key_b, wqkv[1]) + dot_t(d_value_b, wqkv[2])),
        9,
        line=(g_out, g_qkv),
    )
    d_normed1 = flat(d_normed1)
    d_norm1, g_ln1g, g_ln1b = norm_back(x_f, ln1_gain, d_normed1)
    grad_inputs = (d_hidden + d_norm1).astype(bf)

    def line_gather(part):
        whole = lax.all_gather(part, "ctx", axis=0, tiled=False)
        return whole.astype(f32)

    depth = g_proj.shape[1]
    sum_proj = line_gather(g_proj_line.reshape(shards, depth, -1)).transpose(1, 0, 2, 3)
    sum_proj = sum_proj.reshape(shards * units, -1)
    sum_fc = line_gather(g_fc_line.reshape(-1, shards * units)).reshape(-1, shards * units)

    col = t * b_qv.shape[1] + s * width
    g_bqv = jnp.stack([jnp.sum(d_query, axis=0), jnp.sum(d_value, axis=0)])
    full_bqv = lax.dynamic_update_slice(jnp.zeros((2, b_qv.shape[1] * cores), f32), g_bqv, (0, col))
    full_bfc = lax.dynamic_update_slice(
        jnp.zeros((b_fc.shape[0] * cores,), f32), g_bfc, (t * b_fc.shape[0] + s * units,)
    )
    packed = jnp.concatenate(
        [
            full_bqv.reshape(-1),
            full_bfc,
            jnp.sum(d_hidden, axis=0),
            jnp.sum(cot_f, axis=0),
            g_ln1g,
            g_ln1b,
            g_ln2g,
            g_ln2b,
        ]
    )
    filled = packed.size
    tile = shards * cores * 8 * 128
    packed = jnp.pad(packed, (0, -filled % tile)).reshape(shards * cores, -1, 128)
    homes, packed, sum_out, sum_qkv = leave(
        [pieces(outputs), pieces(grad_inputs)], packed, g_out_line, g_qkv_line, 11
    )
    sum_out = sum_out.astype(f32).reshape(shards * width, -1)
    sum_qkv = sum_qkv.astype(f32).reshape(3, -1, shards * width)
    packed = packed.reshape(-1)
    at = full_bqv.size
    sum_bqv = lax.dynamic_slice_in_dim(
        packed[:at].reshape(full_bqv.shape), t * b_qv.shape[1], b_qv.shape[1], axis=1
    )
    sum_bfc = lax.dynamic_slice_in_dim(packed, at + t * b_fc.shape[0], b_fc.shape[0])
    at = at + full_bfc.size
    rest = packed[at : at + 6 * model].reshape(6, model)
    return (
        homes[0].reshape(inputs.shape),
        homes[1].reshape(inputs.shape),
        sum_qkv,
        sum_out,
        sum_fc,
        sum_proj,
        sum_bqv,
        rest[0],
        sum_bfc,
        rest[1],
        rest[2],
        rest[3],
        rest[4],
        rest[5],
    )


def solution(mesh):
    in_specs = (
        P(("shard", "ctx"), None),
        P("shard", None),
        P(("shard", "ctx"), None),
        P(None, "shard", "tp"),
        P("tp", "shard"),
        P("shard", "tp"),
        P("tp", "shard"),
        P(None, "tp"),
        P(),
        P("tp"),
        P(),
        P(),
        P(),
        P(),
        P(),
    )
    out_specs = (
        P(("shard", "ctx"), None),
        P(("shard", "ctx"), None),
        P(None, "shard", "tp"),
        P("tp", "shard"),
        P("shard", "tp"),
        P("tp", "shard"),
        P(None, "tp"),
        P(),
        P("tp"),
        P(),
        P(),
        P(),
        P(),
        P(),
    )
    count = mesh.shape["shard"]
    square = count == mesh.shape["ctx"] and count == 4 and mesh.shape["tp"] == 2
    body = on_device_plane if square else on_device_general
    return jax.shard_map(
        body, mesh=mesh, in_specs=in_specs, out_specs=out_specs, check_vma=False
    )
```
